32 devices in a mesh: grp: 2 (over y), tr: 8 (over z, x), root: 2 (over core).
Axes of the slice: x: 2, y: 2, z: 4, core: 2. Of those that a mesh axis runs over, the one named last changes fastest.
Arguments:
- residual: bfloat16 [128, 65536], P('root', ('grp', 'tr')), parts along dimension 1, may hold values from -8 to 8
- subspace: bfloat16 [512, 65536], P(None, ('grp', 'tr')), parts along dimension 1, may hold values from -1 to 1, as said below
- inverses: bfloat16 [16, 512, 512], P(('grp', 'tr')), parts along dimension 0, may hold values from -1 to 3, as said below
- owner_offset: int32 [128], P(('grp', 'tr')), parts along dimension 0, may hold values from 0 to 3, as said below
- listed: int32 [128], P(('grp', 'tr')), parts along dimension 0, may hold values from 0 to 1, as said below
Outputs:
- corrections: float32 [128, 65536], P('root', ('grp', 'tr')), parts along dimension 1
The draws below stay inside these ranges and needn't reach their ends.
There are 2 independent parts, one for each index of `grp`. The reference program is written for one: setup_inputs(seed, part) draws one part's arguments, and reference() takes and returns one part's arrays. A program takes and returns all parts, laid end to end along the dimension named above; each array names one. Nothing has to cross between parts.
Inputs may be any that keep to these rules, and one draw needn't show every extreme that they name: Each entry of subspace lies within the stated range; rows are not normalized. `inverses`: each inverse is a dense real matrix. `owner_offset`: among the 8 blocks of each shard, at least one is listed and has offset 3. Each shard has at least one listed block and at least one unlisted block.
All inputs are finite; a program needn't handle non-finite values.
Results may differ from the reference program's by a relative error of at most 0.0065.
Values may be sent and summed in bfloat16 or wider, within the bound.
A program may use at most 64 MiB of HBM per device.

```python
import math
import jax
import jax.numpy as jnp
from jax import lax

BLK = 512
R = 128
S = 512
OFFS = 4
PASSES = 2
BLK_DEV = 8
NB = 64
NT = 32768
PAIRS = 8


def subspace_values(key):
    base = jax.random.fold_in(key, 11)
    row_key, common_key, mix_key, scale_key = jax.random.split(base, 4)
    position = jnp.arange(NT, dtype=jnp.float32) / NT
    rows = jax.random.truncated_normal(row_key, -4.0, 4.0, (S, NT), jnp.float32)
    common = jax.random.truncated_normal(common_key, -4.0, 4.0, (8, NT), jnp.float32)
    mixing = jax.random.truncated_normal(mix_key, -4.0, 4.0, (S, 8), jnp.float32) * math.sqrt(0.6 / S)
    scales = jnp.exp(jax.random.uniform(scale_key, (S,), jnp.float32, math.log(0.6), math.log(1.25)))
    envelope = jnp.exp(0.5 * math.log(3.0) * position)
    envelope = envelope / jnp.sqrt(jnp.mean(envelope * envelope))
    entries = rows + jnp.dot(mixing, common, precision=lax.Precision.HIGHEST)
    return entries * envelope[None, :] * scales[:, None] / jnp.sqrt(jnp.float32(NT))


def draw_subspace(key, part):
    return subspace_values(key).astype(jnp.bfloat16)


def draw_residual(key, part):
    basis = subspace_values(key)
    noise_key, weight_key = jax.random.split(jax.random.fold_in(key, 37))
    noise = jax.random.truncated_normal(noise_key, -4.0, 4.0, (R, NT), jnp.float32)
    weights = jax.random.truncated_normal(weight_key, -4.0, 4.0, (R, S), jnp.float32)
    row_norms = jnp.sqrt(jnp.sum(basis * basis, axis=1))
    weights = weights * jnp.sqrt(jnp.float32(NT) / S) / row_norms[None, :]
    values = noise + jnp.dot(weights, basis, precision=lax.Precision.HIGHEST)
    return jnp.clip(values, -8.0, 8.0).astype(jnp.bfloat16)


def draw_inverses(key, part):
    first_key, second_key = jax.random.split(jax.random.fold_in(key, 23))
    diagonal = jnp.exp(jax.random.uniform(first_key, (PAIRS, BLK), jnp.float32, math.log(0.5), math.log(2.0)))
    off_diagonal = jax.random.truncated_normal(second_key, -4.0, 4.0, (PAIRS, BLK, BLK), jnp.float32) * (0.5 / math.sqrt(BLK))
    matrix = off_diagonal + jnp.eye(BLK, dtype=jnp.float32)[None, :, :] * diagonal[:, None, :]
    return matrix.astype(jnp.bfloat16)


def block_plan(key):
    plan_key = jax.random.fold_in(key, 71)
    offset_key, listed_key, forced_key = jax.random.split(plan_key, 3)
    shard_count = NB // BLK_DEV
    offsets = jax.random.randint(offset_key, (NB,), 0, OFFS, dtype=jnp.int32)
    marks = (jax.random.randint(listed_key, (NB,), 0, 8, dtype=jnp.int32) < 7).astype(jnp.int32)
    forced_slot = jax.random.randint(forced_key, (shard_count,), 0, BLK_DEV, dtype=jnp.int32)
    skipped_slot = (forced_slot + 1) % BLK_DEV
    within = jnp.arange(NB, dtype=jnp.int32) % BLK_DEV
    forced = within == jnp.repeat(forced_slot, BLK_DEV)
    skipped = within == jnp.repeat(skipped_slot, BLK_DEV)
    offsets = jnp.where(forced, OFFS - 1, offsets).astype(jnp.int32)
    marks = jnp.where(skipped, 0, marks).astype(jnp.int32)
    marks = jnp.where(forced, 1, marks).astype(jnp.int32)
    return (offsets, marks)


def draw_owner_offset(key, part):
    return block_plan(key)[0]


def draw_listed(key, part):
    return block_plan(key)[1]


def setup_inputs(seed: int = 0, part: int = 0) -> dict:
    splits = jax.random.split(jax.random.key(seed), 6)
    part_keys = jax.random.split(jax.random.fold_in(splits[5], part), 6)
    return {
        "residual": draw_residual(jax.random.fold_in(jax.random.fold_in(splits[5], part), 71), part),
        "subspace": draw_subspace(jax.random.fold_in(jax.random.fold_in(splits[5], part), 71), part),
        "inverses": draw_inverses(jax.random.fold_in(jax.random.fold_in(splits[5], part), 71), part),
        "owner_offset": draw_owner_offset(jax.random.fold_in(jax.random.fold_in(splits[5], part), 71), part),
        "listed": draw_listed(jax.random.fold_in(jax.random.fold_in(splits[5], part), 71), part),
    }


def reference(residual, subspace, inverses, owner_offset, listed):
    block_count = residual.shape[1] // BLK
    blocks = residual.reshape(R, block_count, BLK).transpose(1, 0, 2)
    holder = jnp.arange(block_count, dtype=jnp.int32) // BLK_DEV
    owner_pair = ((holder + owner_offset) % PAIRS).astype(jnp.int32)

    def apply_block(packet):
        residual_block, pair_index, is_listed = packet
        solved = jnp.dot(residual_block, inverses[pair_index], preferred_element_type=jnp.float32)
        return jnp.where(is_listed > 0, solved, residual_block.astype(jnp.float32))

    precond = lax.map(apply_block, (blocks, owner_pair, listed))
    current = precond.transpose(1, 0, 2).reshape(R, block_count * BLK)
    for repeat in range(PASSES):
        rounded = current.astype(jnp.bfloat16)
        correlation = lax.dot_general(rounded, subspace, (((1,), (1,)), ((), ())), preferred_element_type=jnp.float32)
        coefficients = correlation.astype(jnp.bfloat16)
        current = current - jnp.dot(coefficients, subspace, preferred_element_type=jnp.float32)
    return current
```

```python
import functools
import jax
import jax.numpy as jnp
from jax import lax
from jax.experimental import pallas as pl
from jax.experimental.pallas import tpu as pltpu
from jax.sharding import PartitionSpec as P

OFFS = 4
PASSES = 2
SUBLANES = 8
MESH = pl.DeviceIdType.MESH


def each(count, body):
    if count <= 16:
        for i in range(count):
            body(i)
    else:
        pl.loop(0, count)(body)


def kernel(n, roots, off, listed, res, sub, inv, out, table, res_v, sub_v, work, picked,
           partial, inbox, slabs, load_sem, part_send, part_recv, swap_send, swap_recv,
           rs_send, rs_recv, ag_send, ag_recv, out_sem):
    me = lax.axis_index("tr")
    root = lax.axis_index("root")
    rows, cols = res.shape
    blk = inv.shape[1]
    blocks = cols // blk
    spans = sub.shape[0]
    share = blk // roots
    owners = slabs.shape[1]
    slab = rows // owners
    mine = pl.ds(pl.multiple_of(root * share, share), share)

    def block(b):
        return pl.ds(b * blk, blk)

    own_load = pltpu.make_async_copy(inv.at[0], table.at[0], load_sem.at[0])
    own_load.start()
    res_load = pltpu.make_async_copy(res, res_v, load_sem.at[1])
    res_load.start()
    sub_load = pltpu.make_async_copy(sub, sub_v, load_sem.at[2])
    sub_load.start()

    barrier = pltpu.get_barrier_semaphore()

    def greet(d):
        pl.semaphore_signal(barrier, inc=1, device_id={"tr": lax.rem(me + d + 1, n)}, device_id_type=MESH)

    each(n - 1, greet)
    for d in range(1, roots):
        pl.semaphore_signal(barrier, inc=1, device_id={"root": lax.rem(root + d, roots)}, device_id_type=MESH)
    pl.semaphore_wait(barrier, n - 1 + roots - 1)

    def part_copy(o):
        return pltpu.make_async_remote_copy(
            src_ref=inv.at[0, mine], dst_ref=table.at[o, mine],
            send_sem=part_send.at[o], recv_sem=part_recv.at[o],
            device_id={"tr": lax.rem(me + n - o, n)}, device_id_type=MESH)

    def swap_copy(o, d):
        return pltpu.make_async_remote_copy(
            src_ref=table.at[o, mine], dst_ref=table.at[o, mine],
            send_sem=swap_send.at[o, d], recv_sem=swap_recv.at[o, d],
            device_id={"root": lax.rem(root + d, roots)}, device_id_type=MESH)

    def swap_in(o, d):
        other = lax.rem(root + roots - d, roots)
        theirs = pl.ds(pl.multiple_of(other * share, share), share)
        return pltpu.make_async_remote_copy(
            src_ref=table.at[o, theirs], dst_ref=table.at[o, theirs],
            send_sem=swap_send.at[o, d], recv_sem=swap_recv.at[o, d],
            device_id={"root": other}, device_id_type=MESH)

    for o in range(1, OFFS):
        part_copy(o).start()

    res_load.wait()
    for b in range(blocks):
        kept = jnp.where(listed[b] > 0, 0.0, res_v[:, block(b)].astype(jnp.float32))
        work[:, block(b)] = kept

    def apply(o):
        for b in range(blocks):
            hit = jnp.logical_and(listed[b] > 0, off[b] == o)
            x = res_v[:, block(b)].astype(jnp.float32)
            picked[pl.ds(b * rows, rows), :] = jnp.where(hit, x, 0.0).astype(jnp.bfloat16)
        for b in range(blocks):
            part = jnp.dot(picked[pl.ds(b * rows, rows), :], table[o], preferred_element_type=jnp.float32)
            work[:, block(b)] += part

    own_load.wait()
    apply(0)
    for o in range(1, OFFS):
        part_copy(o).wait_recv()
        for d in range(1, roots):
            swap_copy(o, d).start()
        for d in range(1, roots):
            swap_in(o, d).wait_recv()
        apply(o)
    sub_load.wait()

    def rows_of(j):
        return pl.ds(pl.multiple_of(j * slab, slab), slab)

    def rs_copy(k, d):
        peer = lax.rem(me + d + 1, n)
        return peer, pltpu.make_async_remote_copy(
            src_ref=partial.at[k, rows_of(lax.rem(peer, owners))], dst_ref=inbox.at[k, me],
            send_sem=rs_send.at[k, d], recv_sem=rs_recv.at[k, me],
            device_id={"tr": peer}, device_id_type=MESH)

    def rs_in(k, d):
        peer = lax.rem(me + d + 1, n)
        return peer, pltpu.make_async_remote_copy(
            src_ref=inbox.at[k, peer], dst_ref=inbox.at[k, peer],
            send_sem=rs_send.at[k, d], recv_sem=rs_recv.at[k, peer],
            device_id={"tr": peer}, device_id_type=MESH)

    def ag_copy(k, d):
        peer = lax.rem(me + d + 1, n)
        slot = lax.rem(me, owners)
        return peer, pltpu.make_async_remote_copy(
            src_ref=slabs.at[k, slot], dst_ref=slabs.at[k, slot],
            send_sem=ag_send.at[k, d], recv_sem=ag_recv.at[k, slot],
            device_id={"tr": peer}, device_id_type=MESH)

    def ag_in(k, peer):
        slot = lax.rem(peer, owners)
        return pltpu.make_async_remote_copy(
            src_ref=slabs.at[k, slot], dst_ref=slabs.at[k, slot],
            send_sem=ag_send.at[k, 0], recv_sem=ag_recv.at[k, slot],
            device_id={"tr": peer}, device_id_type=MESH)

    def only(test, body):
        if owners == n:
            body()
        else:
            pl.when(test)(body)

    for k in range(PASSES):
        total = jnp.zeros((rows, spans), jnp.float32)
        for b in range(blocks):
            total += lax.dot_general(
                work[:, block(b)].astype(jnp.bfloat16), sub_v[:, block(b)],
                (((1,), (1,)), ((), ())), preferred_element_type=jnp.float32)
        partial[k] = total

        def send_partial(d):
            peer, copy = rs_copy(k, d)
            only(peer < owners, copy.start)

        each(n - 1, send_partial)

        def own_sum():
            inbox[k, me] = partial[k, rows_of(lax.rem(me, owners))]

            def arrive(d):
                rs_in(k, d)[1].wait_recv()

            each(n - 1, arrive)
            slabs[k, lax.rem(me, owners)] = jnp.sum(inbox[k], axis=0).astype(jnp.bfloat16)

            def spread(d):
                ag_copy(k, d)[1].start()

            each(n - 1, spread)

        only(me < owners, own_sum)

        def gather(d):
            peer = lax.rem(me + d + 1, n)
            only(peer < owners, lambda: ag_in(k, peer).wait_recv())

        each(n - 1, gather)
        coef = jnp.concatenate(
            [slabs[k, j].astype(jnp.float32) for j in range(owners)], axis=0).astype(jnp.bfloat16)
        for b in range(blocks):
            work[:, block(b)] -= jnp.dot(coef, sub_v[:, block(b)], preferred_element_type=jnp.float32)
            if k == PASSES - 1:
                pltpu.make_async_copy(work.at[:, block(b)], out.at[:, block(b)], out_sem.at[b]).start()

    for o in range(1, OFFS):
        part_copy(o).wait_send()
        for d in range(1, roots):
            swap_copy(o, d).wait_send()
    for k in range(PASSES):

        def drain(d):
            peer, copy = rs_copy(k, d)
            only(peer < owners, copy.wait_send)
            only(me < owners, ag_copy(k, d)[1].wait_send)

        each(n - 1, drain)
    for b in range(blocks):
        pltpu.make_async_copy(work.at[:, block(b)], out.at[:, block(b)], out_sem.at[b]).wait()


def per_device(n, roots, residual, subspace, inverses, owner_offset, listed):
    rows, cols = residual.shape
    spans = subspace.shape[0]
    blk = inverses.shape[1]
    blocks = cols // blk
    owners = min(n, rows // SUBLANES)
    slab = rows // owners
    hbm = pl.BlockSpec(memory_space=pl.ANY)
    smem = pl.BlockSpec(memory_space=pltpu.SMEM)
    dma = pltpu.SemaphoreType.DMA
    return pl.pallas_call(
        functools.partial(kernel, n, roots),
        out_shape=jax.ShapeDtypeStruct((rows, cols), jnp.float32),
        in_specs=[smem, smem, hbm, hbm, hbm],
        out_specs=hbm,
        scratch_shapes=[
            pltpu.VMEM((OFFS, blk, blk), jnp.bfloat16),
            pltpu.VMEM((rows, cols), jnp.bfloat16),
            pltpu.VMEM((spans, cols), jnp.bfloat16),
            pltpu.VMEM((rows, cols), jnp.float32),
            pltpu.VMEM((blocks * rows, blk), jnp.bfloat16),
            pltpu.VMEM((PASSES, rows, spans), jnp.float32),
            pltpu.VMEM((PASSES, n, slab, spans), jnp.float32),
            pltpu.VMEM((PASSES, owners, slab, spans), jnp.bfloat16),
            dma((3,)),
            dma((OFFS,)), dma((OFFS,)),
            dma((OFFS, roots)), dma((OFFS, roots)),
            dma((PASSES, n)), dma((PASSES, n)),
            dma((PASSES, n)), dma((PASSES, owners)),
            dma((blocks,)),
        ],
        compiler_params=pltpu.CompilerParams(collective_id=0, has_side_effects=True),
    )(owner_offset, listed, residual, subspace, inverses)


def solution(mesh):
    body = functools.partial(per_device, mesh.shape["tr"], mesh.shape["root"])
    return jax.shard_map(
        body,
        mesh=mesh,
        in_specs=(
            P("root", ("grp", "tr")),
            P(None, ("grp", "tr")),
            P(("grp", "tr"), None, None),
            P(("grp", "tr")),
            P(("grp", "tr")),
        ),
        out_specs=P("root", ("grp", "tr")),
        check_vma=False,
    )
```

```python
import functools
import jax
import jax.numpy as jnp
from jax import lax
from jax.experimental import pallas as pl
from jax.experimental.pallas import tpu as pltpu
from jax.sharding import PartitionSpec as P

OFFS = 4
PASSES = 2
SUBLANES = 8
CHUNKS = 2
HOPS = 6
MESH = pl.DeviceIdType.MESH


def each(count, body):
    if count <= 16:
        for i in range(count):
            body(i)
    else:
        pl.loop(0, count)(body)


def kernel(n, roots, off, listed, res, sub, inv, out, table, res_v, sub_v, work, picked,
           partial, inbox, slabs, load_sem, hop_send, hop_recv, swap_send, swap_recv,
           rs_send, rs_recv, ag_send, ag_recv, out_sem):
    me = lax.axis_index("tr")
    root = lax.axis_index("root")
    rows, cols = res.shape
    blk = inv.shape[1]
    blocks = cols // blk
    spans = sub.shape[0]
    share = blk // roots
    owners = slabs.shape[1]
    slab = rows // owners

    def block(b):
        return pl.ds(b * blk, blk)

    own_load = pltpu.make_async_copy(inv.at[0], table.at[lax.rem(me, 2)], load_sem.at[0])
    own_load.start()
    res_load = pltpu.make_async_copy(res, res_v, load_sem.at[1])
    res_load.start()
    sub_load = pltpu.make_async_copy(sub, sub_v, load_sem.at[2])
    sub_load.start()

    barrier = pltpu.get_barrier_semaphore()

    def greet(d):
        pl.semaphore_signal(barrier, inc=1, device_id={"tr": lax.rem(me + d + 1, n)}, device_id_type=MESH)

    each(n - 1, greet)
    for d in range(1, roots):
        pl.semaphore_signal(barrier, inc=1, device_id={"root": lax.rem(root + d, roots)}, device_id_type=MESH)
    pl.semaphore_wait(barrier, n - 1 + roots - 1)

    side = lax.rem(me, 2)
    chunk = share // CHUNKS

    def chunk_rows(half, q):
        return pl.ds(pl.multiple_of(half * share + q * chunk, chunk), chunk)

    def hop(src, q, slot, peer, sem):
        return pltpu.make_async_remote_copy(
            src_ref=src, dst_ref=table.at[slot, chunk_rows(root, q)],
            send_sem=hop_send.at[sem, q], recv_sem=hop_recv.at[slot, q],
            device_id={"tr": lax.rem(peer + n, n)}, device_id_type=MESH)

    def own_hop(q, slot, peer, sem):
        return hop(inv.at[0, chunk_rows(root, q)], q, slot, peer, sem)

    def relay(e, q, slot, peer, sem):
        return hop(table.at[e, chunk_rows(root, q)], q, slot, peer, sem)

    def swap(e, q, half):
        rows_q = table.at[e, chunk_rows(half, q)]
        return pltpu.make_async_remote_copy(
            src_ref=rows_q, dst_ref=rows_q,
            send_sem=swap_send.at[e, q], recv_sem=swap_recv.at[e, q],
            device_id={"root": 1 - root}, device_id_type=MESH)

    twin = me + 1 - 2 * side
    near = me - 2
    far = me - 4
    roles = {
        (0, 0): ([(2, near), (4, far)], [(1, [(3, near)]), (2, [(2, twin)]), (4, [(4, twin)]), (3, [(3, twin)])]),
        (1, 1): ([(3, near), (1, twin)], [(0, [(2, near), (4, far)]), (3, [(3, twin)]), (2, [(2, twin)]), (4, [])]),
        (1, 0): ([(1, twin)], [(2, []), (4, []), (3, [])]),
        (0, 1): ([(0, twin)], [(1, []), (3, []), (2, [])]),
    }

    def per_role(body):
        for (s, r), (own, events) in roles.items():
            pl.when(jnp.logical_and(side == s, root == r))(functools.partial(body, s, own, events))

    def sem_of(events, i, j):
        return 2 + sum(len(targets) for _, targets in events[:i]) + j

    def open_hops(s, own, events):
        for j, (slot, peer) in enumerate(own):
            for q in range(CHUNKS):
                own_hop(q, slot, peer, j).start()

    def run_events(first, s, own, events):
        cut = len(events) - 1
        for i, (e, targets) in enumerate(events):
            if (i < cut) != first:
                continue
            for q in range(CHUNKS):
                relay(e, q, e, twin, 0).wait_recv()
                for j, (slot, peer) in enumerate(targets):
                    relay(e, q, slot, peer, sem_of(events, i, j)).start()
                if s < e < s + OFFS:
                    swap(e, q, root).start()

    def close_hops(s, own, events):
        for j, (slot, peer) in enumerate(own):
            for q in range(CHUNKS):
                own_hop(q, slot, peer, j).wait_send()
        for i, (e, targets) in enumerate(events):
            for q in range(CHUNKS):
                for j, (slot, peer) in enumerate(targets):
                    relay(e, q, slot, peer, sem_of(events, i, j)).wait_send()
                if s < e < s + OFFS:
                    swap(e, q, root).wait_send()

    per_role(open_hops)

    res_load.wait()
    for b in range(blocks):
        kept = jnp.where(listed[b] > 0, 0.0, res_v[:, block(b)].astype(jnp.float32))
        work[:, block(b)] = kept

    def apply(o):
        for b in range(blocks):
            hit = jnp.logical_and(listed[b] > 0, off[b] == o)
            x = res_v[:, block(b)].astype(jnp.float32)
            picked[pl.ds(b * rows, rows), :] = jnp.where(hit, x, 0.0).astype(jnp.bfloat16)
        for b in range(blocks):
            part = jnp.dot(picked[pl.ds(b * rows, rows), :], table[side + o], preferred_element_type=jnp.float32)
            work[:, block(b)] += part

    def arrive_and_apply(o):
        for q in range(CHUNKS):
            swap(side + o, q, 1 - root).wait_recv()
        apply(o)

    own_load.wait()
    apply(0)
    per_role(functools.partial(run_events, True))
    arrive_and_apply(1)
    per_role(functools.partial(run_events, False))
    for o in range(2, OFFS):
        arrive_and_apply(o)
    sub_load.wait()

    def rows_of(j):
        return pl.ds(pl.multiple_of(j * slab, slab), slab)

    def rs_copy(k, d):
        peer = lax.rem(me + d + 1, n)
        return peer, pltpu.make_async_remote_copy(
            src_ref=partial.at[k, rows_of(lax.rem(peer, owners))], dst_ref=inbox.at[k, me],
            send_sem=rs_send.at[k, d], recv_sem=rs_recv.at[k, me],
            device_id={"tr": peer}, device_id_type=MESH)

    def rs_in(k, d):
        peer = lax.rem(me + d + 1, n)
        return peer, pltpu.make_async_remote_copy(
            src_ref=inbox.at[k, peer], dst_ref=inbox.at[k, peer],
            send_sem=rs_send.at[k, d], recv_sem=rs_recv.at[k, peer],
            device_id={"tr": peer}, device_id_type=MESH)

    def ag_copy(k, d):
        peer = lax.rem(me + d + 1, n)
        slot = lax.rem(me, owners)
        return peer, pltpu.make_async_remote_copy(
            src_ref=slabs.at[k, slot], dst_ref=slabs.at[k, slot],
            send_sem=ag_send.at[k, d], recv_sem=ag_recv.at[k, slot],
            device_id={"tr": peer}, device_id_type=MESH)

    def ag_in(k, peer):
        slot = lax.rem(peer, owners)
        return pltpu.make_async_remote_copy(
            src_ref=slabs.at[k, slot], dst_ref=slabs.at[k, slot],
            send_sem=ag_send.at[k, 0], recv_sem=ag_recv.at[k, slot],
            device_id={"tr": peer}, device_id_type=MESH)

    def only(test, body):
        if owners == n:
            body()
        else:
            pl.when(test)(body)

    for k in range(PASSES):
        total = jnp.zeros((rows, spans), jnp.float32)
        for b in range(blocks):
            total += lax.dot_general(
                work[:, block(b)].astype(jnp.bfloat16), sub_v[:, block(b)],
                (((1,), (1,)), ((), ())), preferred_element_type=jnp.float32)
        partial[k] = total

        def send_partial(d):
            peer, copy = rs_copy(k, d)
            only(peer < owners, copy.start)

        each(n - 1, send_partial)

        def own_sum():
            inbox[k, me] = partial[k, rows_of(lax.rem(me, owners))]

            def arrive(d):
                rs_in(k, d)[1].wait_recv()

            each(n - 1, arrive)
            slabs[k, lax.rem(me, owners)] = jnp.sum(inbox[k], axis=0).astype(jnp.bfloat16)

            def spread(d):
                ag_copy(k, d)[1].start()

            each(n - 1, spread)

        only(me < owners, own_sum)

        def gather(d):
            peer = lax.rem(me + d + 1, n)
            only(peer < owners, lambda: ag_in(k, peer).wait_recv())

        each(n - 1, gather)
        coef = jnp.concatenate(
            [slabs[k, j].astype(jnp.float32) for j in range(owners)], axis=0).astype(jnp.bfloat16)
        for b in range(blocks):
            work[:, block(b)] -= jnp.dot(coef, sub_v[:, block(b)], preferred_element_type=jnp.float32)
            if k == PASSES - 1:
                pltpu.make_async_copy(work.at[:, block(b)], out.at[:, block(b)], out_sem.at[b]).start()

    per_role(close_hops)
    for k in range(PASSES):

        def drain(d):
            peer, copy = rs_copy(k, d)
            only(peer < owners, copy.wait_send)
            only(me < owners, ag_copy(k, d)[1].wait_send)

        each(n - 1, drain)
    for b in range(blocks):
        pltpu.make_async_copy(work.at[:, block(b)], out.at[:, block(b)], out_sem.at[b]).wait()


def per_device(n, roots, residual, subspace, inverses, owner_offset, listed):
    rows, cols = residual.shape
    spans = subspace.shape[0]
    blk = inverses.shape[1]
    blocks = cols // blk
    owners = min(n, rows // SUBLANES)
    slab = rows // owners
    hbm = pl.BlockSpec(memory_space=pl.ANY)
    smem = pl.BlockSpec(memory_space=pltpu.SMEM)
    dma = pltpu.SemaphoreType.DMA
    return pl.pallas_call(
        functools.partial(kernel, n, roots),
        out_shape=jax.ShapeDtypeStruct((rows, cols), jnp.float32),
        in_specs=[smem, smem, hbm, hbm, hbm],
        out_specs=hbm,
        scratch_shapes=[
            pltpu.VMEM((OFFS + 1, blk, blk), jnp.bfloat16),
            pltpu.VMEM((rows, cols), jnp.bfloat16),
            pltpu.VMEM((spans, cols), jnp.bfloat16),
            pltpu.VMEM((rows, cols), jnp.float32),
            pltpu.VMEM((blocks * rows, blk), jnp.bfloat16),
            pltpu.VMEM((PASSES, rows, spans), jnp.float32),
            pltpu.VMEM((PASSES, n, slab, spans), jnp.float32),
            pltpu.VMEM((PASSES, owners, slab, spans), jnp.bfloat16),
            dma((3,)),
            dma((HOPS, CHUNKS)), dma((OFFS + 1, CHUNKS)),
            dma((OFFS + 1, CHUNKS)), dma((OFFS + 1, CHUNKS)),
            dma((PASSES, n)), dma((PASSES, n)),
            dma((PASSES, n)), dma((PASSES, owners)),
            dma((blocks,)),
        ],
        compiler_params=pltpu.CompilerParams(collective_id=0, has_side_effects=True),
    )(owner_offset, listed, residual, subspace, inverses)


def solution(mesh):
    body = functools.partial(per_device, mesh.shape["tr"], mesh.shape["root"])
    return jax.shard_map(
        body,
        mesh=mesh,
        in_specs=(
            P("root", ("grp", "tr")),
            P(None, ("grp", "tr")),
            P(("grp", "tr"), None, None),
            P(("grp", "tr")),
            P(("grp", "tr")),
        ),
        out_specs=P("root", ("grp", "tr")),
        check_vma=False,
    )
```

```python
import functools
import jax
import jax.numpy as jnp
from jax import lax
from jax.experimental import pallas as pl
from jax.experimental.pallas import tpu as pltpu
from jax.sharding import PartitionSpec as P

OFFS = 4
PASSES = 2
PARTS = 1
LINK = jnp.bfloat16
SUBLANES = 8
CHUNKS = 4
HOPS = 6
MESH = pl.DeviceIdType.MESH


def each(count, body):
    if count <= 16:
        for i in range(count):
            body(i)
    else:
        pl.loop(0, count)(body)


def kernel(n, roots, off, listed, res, sub, inv, out, table, res_v, sub_v, work, picked,
           partial, inbox, slabs, load_sem, hop_send, hop_recv, swap_send, swap_recv,
           rs_send, rs_recv, ag_send, ag_recv, out_sem):
    me = lax.axis_index("tr")
    root = lax.axis_index("root")
    rows, cols = res.shape
    blk = inv.shape[1]
    blocks = cols // blk
    width = sub.shape[0] // PARTS
    share = blk // roots
    owners = slabs.shape[1]
    base = (n - owners) // 2
    slab = rows // owners

    def block(b):
        return pl.ds(b * blk, blk)

    own_load = pltpu.make_async_copy(inv.at[0], table.at[lax.rem(me, 2)], load_sem.at[0])
    own_load.start()
    res_load = pltpu.make_async_copy(res, res_v, load_sem.at[1])
    res_load.start()
    sub_load = pltpu.make_async_copy(sub, sub_v, load_sem.at[2])
    sub_load.start()

    barrier = pltpu.get_barrier_semaphore()

    def is_owner(device):
        return jnp.logical_and(device >= base, device < base + owners)

    side = lax.rem(me, 2)
    twin = me + 1 - 2 * side

    def linked(d):
        peer = lax.rem(me + d + 1, n)
        close = jnp.logical_or(jnp.logical_or(d + 1 == 2, d + 1 == n - 2), peer == twin)
        return jnp.logical_or(close, jnp.logical_or(is_owner(me), is_owner(peer)))

    def greet(d):
        def signal():
            pl.semaphore_signal(barrier, inc=1, device_id={"tr": lax.rem(me + d + 1, n)}, device_id_type=MESH)

        pl.when(linked(d))(signal)

    each(n - 1, greet)
    for d in range(1, roots):
        pl.semaphore_signal(barrier, inc=1, device_id={"root": lax.rem(root + d, roots)}, device_id_type=MESH)
    partners = lax.fori_loop(0, n - 1, lambda d, c: c + linked(d).astype(jnp.int32), jnp.int32(roots - 1))
    pl.semaphore_wait(barrier, partners)

    chunk = share // CHUNKS

    def chunk_rows(half, q):
        return pl.ds(pl.multiple_of(half * share + q * chunk, chunk), chunk)

    def hop(src, q, slot, peer, sem):
        return pltpu.make_async_remote_copy(
            src_ref=src, dst_ref=table.at[slot, chunk_rows(root, q)],
            send_sem=hop_send.at[sem, q], recv_sem=hop_recv.at[slot, q],
            device_id={"tr": lax.rem(peer + n, n)}, device_id_type=MESH)

    def own_hop(q, slot, peer, sem):
        return hop(inv.at[0, chunk_rows(root, q)], q, slot, peer, sem)

    def relay(e, q, slot, peer, sem):
        return hop(table.at[e, chunk_rows(root, q)], q, slot, peer, sem)

    def swap(e, q, half):
        rows_q = table.at[e, chunk_rows(half, q)]
        return pltpu.make_async_remote_copy(
            src_ref=rows_q, dst_ref=rows_q,
            send_sem=swap_send.at[e, q], recv_sem=swap_recv.at[e, q],
            device_id={"root": 1 - root}, device_id_type=MESH)

    near = me - 2
    roles = {
        (0, 0): ([(2, near)], [(1, [(3, near)], []), (2, [(4, near), (2, twin)], []), (3, [(3, twin)], []), (4, [(4, twin)], [])]),
        (1, 1): ([(3, near)], [(0, [(2, near)], [(1, twin)]), (3, [(3, twin)], []), (2, [(4, near), (2, twin)], []), (4, [], [])]),
        (1, 0): ([(1, twin)], [(2, [], []), (3, [], []), (4, [], [])]),
        (0, 1): ([(0, twin)], [(1, [], []), (3, [], []), (2, [], [])]),
    }

    def per_role(body):
        for (s, r), (own, events) in roles.items():
            pl.when(jnp.logical_and(side == s, root == r))(functools.partial(body, s, own, events))

    def sem_of(events, i, j):
        return 1 + sum(len(targets) + len(late) for _, targets, late in events[:i]) + j

    def open_hops(s, own, events):
        for j, (slot, peer) in enumerate(own):
            for q in range(CHUNKS):
                own_hop(q, slot, peer, j).start()

    def run_events(first, s, own, events):
        cut = len(events) - 1
        for i, (e, targets, late) in enumerate(events):
            if (i < cut) != first:
                continue
            for q in range(CHUNKS):
                relay(e, q, e, twin, 0).wait_recv()
                for j, (slot, peer) in enumerate(targets):
                    relay(e, q, slot, peer, sem_of(events, i, j)).start()
                for j, (slot, peer) in enumerate(late):
                    own_hop(q, slot, peer, sem_of(events, i, len(targets) + j)).start()
                if s < e < s + OFFS:
                    swap(e, q, root).start()

    def close_hops(s, own, events):
        for j, (slot, peer) in enumerate(own):
            for q in range(CHUNKS):
                own_hop(q, slot, peer, j).wait_send()
        for i, (e, targets, late) in enumerate(events):
            for q in range(CHUNKS):
                for j, (slot, peer) in enumerate(targets):
                    relay(e, q, slot, peer, sem_of(events, i, j)).wait_send()
                for j, (slot, peer) in enumerate(late):
                    own_hop(q, slot, peer, sem_of(events, i, len(targets) + j)).wait_send()
                if s < e < s + OFFS:
                    swap(e, q, root).wait_send()

    per_role(open_hops)

    res_load.wait()
    for b in range(blocks):
        kept = jnp.where(listed[b] > 0, 0.0, res_v[:, block(b)].astype(jnp.float32))
        work[:, block(b)] = kept

    def apply(o):
        for b in range(blocks):
            hit = jnp.logical_and(listed[b] > 0, off[b] == o)
            x = res_v[:, block(b)].astype(jnp.float32)
            picked[pl.ds(b * rows, rows), :] = jnp.where(hit, x, 0.0).astype(jnp.bfloat16)
        for b in range(blocks):
            part = jnp.dot(picked[pl.ds(b * rows, rows), :], table[side + o], preferred_element_type=jnp.float32)
            work[:, block(b)] += part

    def arrive_and_apply(o):
        for q in range(CHUNKS):
            swap(side + o, q, 1 - root).wait_recv()
        apply(o)

    own_load.wait()
    apply(0)
    per_role(functools.partial(run_events, True))
    arrive_and_apply(1)
    per_role(functools.partial(run_events, False))
    for o in range(2, OFFS):
        arrive_and_apply(o)
    sub_load.wait()

    def rs_copy(i, j):
        return pltpu.make_async_remote_copy(
            src_ref=partial.at[i, j], dst_ref=inbox.at[i, me],
            send_sem=rs_send.at[i, j], recv_sem=rs_recv.at[i, me],
            device_id={"tr": base + j}, device_id_type=MESH)

    def rs_in(i, peer):
        return pltpu.make_async_remote_copy(
            src_ref=inbox.at[i, peer], dst_ref=inbox.at[i, peer],
            send_sem=rs_send.at[i, 0], recv_sem=rs_recv.at[i, peer],
            device_id={"tr": peer}, device_id_type=MESH)

    def ag_copy(i, d):
        return pltpu.make_async_remote_copy(
            src_ref=slabs.at[i, me - base], dst_ref=slabs.at[i, me - base],
            send_sem=ag_send.at[i, d], recv_sem=ag_recv.at[i, me - base],
            device_id={"tr": lax.rem(me + d + 1, n)}, device_id_type=MESH)

    def ag_in(i, j):
        return pltpu.make_async_remote_copy(
            src_ref=slabs.at[i, j], dst_ref=slabs.at[i, j],
            send_sem=ag_send.at[i, 0], recv_sem=ag_recv.at[i, j],
            device_id={"tr": base + j}, device_id_type=MESH)

    def span(h):
        return pl.ds(h * width, width)

    def for_other_owners(body):
        for j in range(owners):
            pl.when(me != base + j)(functools.partial(body, j))

    for k in range(PASSES):
        for b in range(blocks):
            res_v[:, block(b)] = work[:, block(b)].astype(jnp.bfloat16)
        for h in range(PARTS):
            i = k * PARTS + h
            total = jnp.zeros((rows, width), jnp.float32)
            for b in range(blocks):
                total += lax.dot_general(
                    res_v[:, block(b)], sub_v[span(h), block(b)],
                    (((1,), (1,)), ((), ())), preferred_element_type=jnp.float32)
            partial[i] = total.reshape(owners, slab, width).astype(partial.dtype)

            for_other_owners(lambda j: rs_copy(i, j).start())

        def own_sum(i):
            inbox[i, me] = partial[i, me - base]
            each(n - 1, lambda d: rs_in(i, lax.rem(me + d + 1, n)).wait_recv())
            slabs[i, me - base] = jnp.sum(inbox[i].astype(jnp.float32), axis=0).astype(jnp.bfloat16)
            each(n - 1, lambda d: ag_copy(i, d).start())

        for h in range(PARTS):
            pl.when(is_owner(me))(functools.partial(own_sum, k * PARTS + h))
        for h in range(PARTS):
            i = k * PARTS + h
            for_other_owners(lambda j: ag_in(i, j).wait_recv())
            coef = jnp.concatenate(
                [slabs[i, j].astype(jnp.float32) for j in range(owners)], axis=0).astype(jnp.bfloat16)
            for b in range(blocks):
                work[:, block(b)] -= jnp.dot(
                    coef, sub_v[span(h), block(b)], preferred_element_type=jnp.float32)
                if i == PASSES * PARTS - 1:
                    pltpu.make_async_copy(work.at[:, block(b)], out.at[:, block(b)], out_sem.at[b]).start()

    per_role(close_hops)
    for i in range(PASSES * PARTS):
        for_other_owners(lambda j: rs_copy(i, j).wait_send())

        def sent():
            each(n - 1, lambda d: ag_copy(i, d).wait_send())

        pl.when(is_owner(me))(sent)
    for b in range(blocks):
        pltpu.make_async_copy(work.at[:, block(b)], out.at[:, block(b)], out_sem.at[b]).wait()


def per_device(n, roots, residual, subspace, inverses, owner_offset, listed):
    rows, cols = residual.shape
    spans = subspace.shape[0]
    blk = inverses.shape[1]
    blocks = cols // blk
    owners = min(n // 2, rows // SUBLANES)
    slab = rows // owners
    rounds = PASSES * PARTS
    hbm = pl.BlockSpec(memory_space=pl.ANY)
    smem = pl.BlockSpec(memory_space=pltpu.SMEM)
    dma = pltpu.SemaphoreType.DMA
    return pl.pallas_call(
        functools.partial(kernel, n, roots),
        out_shape=jax.ShapeDtypeStruct((rows, cols), jnp.float32),
        in_specs=[smem, smem, hbm, hbm, hbm],
        out_specs=hbm,
        scratch_shapes=[
            pltpu.VMEM((OFFS + 1, blk, blk), jnp.bfloat16),
            pltpu.VMEM((rows, cols), jnp.bfloat16),
            pltpu.VMEM((spans, cols), jnp.bfloat16),
            pltpu.VMEM((rows, cols), jnp.float32),
            pltpu.VMEM((blocks * rows, blk), jnp.bfloat16),
            pltpu.VMEM((rounds, owners, slab, spans // PARTS), LINK),
            pltpu.VMEM((rounds, n, slab, spans // PARTS), LINK),
            pltpu.VMEM((rounds, owners, slab, spans // PARTS), jnp.bfloat16),
            dma((3,)),
            dma((HOPS, CHUNKS)), dma((OFFS + 1, CHUNKS)),
            dma((OFFS + 1, CHUNKS)), dma((OFFS + 1, CHUNKS)),
            dma((rounds, owners)), dma((rounds, n)),
            dma((rounds, n)), dma((rounds, owners)),
            dma((blocks,)),
        ],
        compiler_params=pltpu.CompilerParams(collective_id=0, has_side_effects=True),
    )(owner_offset, listed, residual, subspace, inverses)


def solution(mesh):
    body = functools.partial(per_device, mesh.shape["tr"], mesh.shape["root"])
    return jax.shard_map(
        body,
        mesh=mesh,
        in_specs=(
            P("root", ("grp", "tr")),
            P(None, ("grp", "tr")),
            P(("grp", "tr"), None, None),
            P(("grp", "tr")),
            P(("grp", "tr")),
        ),
        out_specs=P("root", ("grp", "tr")),
        check_vma=False,
    )
```

```python
import functools
import jax
import jax.numpy as jnp
from jax import lax
from jax.experimental import pallas as pl
from jax.experimental.pallas import tpu as pltpu
from jax.sharding import PartitionSpec as P

OFFS = 4
PASSES = 2
PARTS = 1
LINK = jnp.bfloat16
SUBLANES = 8
CHUNKS = 4
HOPS = 6
MESH = pl.DeviceIdType.MESH


def each(count, body):
    if count <= 16:
        for i in range(count):
            body(i)
    else:
        pl.loop(0, count)(body)


def kernel(n, roots, off, listed, res, sub, inv, out, table, res_v, sub_v, work, picked,
           partial, inbox, slabs, load_sem, hop_send, hop_recv, swap_send, swap_recv,
           rs_send, rs_recv, ag_send, ag_recv, out_sem):
    me = lax.axis_index("tr")
    root = lax.axis_index("root")
    rows, cols = res.shape
    blk = inv.shape[1]
    blocks = cols // blk
    width = sub.shape[0] // PARTS
    share = blk // roots
    owners = slabs.shape[1]
    base = (n - owners) // 2
    slab = rows // owners

    def block(b):
        return pl.ds(b * blk, blk)

    own_load = pltpu.make_async_copy(inv.at[0], table.at[lax.rem(me, 2)], load_sem.at[0])
    own_load.start()
    res_load = pltpu.make_async_copy(res, res_v, load_sem.at[1])
    res_load.start()
    sub_load = pltpu.make_async_copy(sub, sub_v, load_sem.at[2])
    sub_load.start()

    barrier = pltpu.get_barrier_semaphore()

    def is_owner(device):
        return jnp.logical_and(device >= base, device < base + owners)

    side = lax.rem(me, 2)
    twin = me + 1 - 2 * side

    def linked(d):
        peer = lax.rem(me + d + 1, n)
        close = jnp.logical_or(jnp.logical_or(d + 1 == 2, d + 1 == n - 2), peer == twin)
        return jnp.logical_or(close, jnp.logical_or(is_owner(me), is_owner(peer)))

    def greet(d):
        def signal():
            pl.semaphore_signal(barrier, inc=1, device_id={"tr": lax.rem(me + d + 1, n)}, device_id_type=MESH)

        pl.when(linked(d))(signal)

    each(n - 1, greet)
    for d in range(1, roots):
        pl.semaphore_signal(barrier, inc=1, device_id={"root": lax.rem(root + d, roots)}, device_id_type=MESH)
    partners = lax.fori_loop(0, n - 1, lambda d, c: c + linked(d).astype(jnp.int32), jnp.int32(roots - 1))
    pl.semaphore_wait(barrier, partners)

    chunk = share // CHUNKS

    def chunk_rows(half, q):
        return pl.ds(pl.multiple_of(half * share + q * chunk, chunk), chunk)

    def hop(src, q, slot, peer, sem):
        return pltpu.make_async_remote_copy(
            src_ref=src, dst_ref=table.at[slot, chunk_rows(root, q)],
            send_sem=hop_send.at[sem, q], recv_sem=hop_recv.at[slot, q],
            device_id={"tr": lax.rem(peer + n, n)}, device_id_type=MESH)

    def own_hop(q, slot, peer, sem):
        return hop(inv.at[0, chunk_rows(root, q)], q, slot, peer, sem)

    def relay(e, q, slot, peer, sem):
        return hop(table.at[e, chunk_rows(root, q)], q, slot, peer, sem)

    def swap(e, q, half):
        rows_q = table.at[e, chunk_rows(half, q)]
        return pltpu.make_async_remote_copy(
            src_ref=rows_q, dst_ref=rows_q,
            send_sem=swap_send.at[e, q], recv_sem=swap_recv.at[e, q],
            device_id={"root": 1 - root}, device_id_type=MESH)

    near = me - 2
    roles = {
        (0, 0): ([(2, near)], [(1, [(3, near)], []), (2, [(4, near), (2, twin)], []), (3, [(3, twin)], []), (4, [(4, twin)], [])]),
        (1, 1): ([(3, near)], [(0, [(2, near)], []), (3, [(3, twin)], [(1, twin)]), (2, [(4, near), (2, twin)], []), (4, [], [])]),
        (1, 0): ([(1, twin)], [(2, [], []), (3, [], []), (4, [], [])]),
        (0, 1): ([(0, twin)], [(1, [], []), (3, [], []), (2, [], [])]),
    }

    def per_role(body):
        for (s, r), (own, events) in roles.items():
            pl.when(jnp.logical_and(side == s, root == r))(functools.partial(body, s, own, events))

    def sem_of(events, i, j):
        return 1 + sum(len(targets) + len(late) for _, targets, late in events[:i]) + j

    def open_hops(s, own, events):
        for j, (slot, peer) in enumerate(own):
            for q in range(CHUNKS):
                own_hop(q, slot, peer, j).start()

    def run_events(first, s, own, events):
        cut = len(events) - 1
        for i, (e, targets, late) in enumerate(events):
            if (i < cut) != first:
                continue
            for q in range(CHUNKS):
                relay(e, q, e, twin, 0).wait_recv()
                for j, (slot, peer) in enumerate(targets):
                    relay(e, q, slot, peer, sem_of(events, i, j)).start()
                for j, (slot, peer) in enumerate(late):
                    own_hop(q, slot, peer, sem_of(events, i, len(targets) + j)).start()
                if s < e < s + OFFS:
                    swap(e, q, root).start()

    def close_hops(s, own, events):
        for j, (slot, peer) in enumerate(own):
            for q in range(CHUNKS):
                own_hop(q, slot, peer, j).wait_send()
        for i, (e, targets, late) in enumerate(events):
            for q in range(CHUNKS):
                for j, (slot, peer) in enumerate(targets):
                    relay(e, q, slot, peer, sem_of(events, i, j)).wait_send()
                for j, (slot, peer) in enumerate(late):
                    own_hop(q, slot, peer, sem_of(events, i, len(targets) + j)).wait_send()
                if s < e < s + OFFS:
                    swap(e, q, root).wait_send()

    per_role(open_hops)

    res_load.wait()
    for b in range(blocks):
        kept = jnp.where(listed[b] > 0, 0.0, res_v[:, block(b)].astype(jnp.float32))
        work[:, block(b)] = kept

    def apply(o):
        for b in range(blocks):
            hit = jnp.logical_and(listed[b] > 0, off[b] == o)
            x = res_v[:, block(b)].astype(jnp.float32)
            picked[pl.ds(b * rows, rows), :] = jnp.where(hit, x, 0.0).astype(jnp.bfloat16)
        for b in range(blocks):
            part = jnp.dot(picked[pl.ds(b * rows, rows), :], table[side + o], preferred_element_type=jnp.float32)
            work[:, block(b)] += part

    def arrive_and_apply(o):
        for q in range(CHUNKS):
            swap(side + o, q, 1 - root).wait_recv()
        apply(o)

    own_load.wait()
    apply(0)
    per_role(functools.partial(run_events, True))
    arrive_and_apply(1)
    per_role(functools.partial(run_events, False))
    for o in range(2, OFFS):
        arrive_and_apply(o)
    sub_load.wait()

    def rs_copy(i, j):
        return pltpu.make_async_remote_copy(
            src_ref=partial.at[i, j], dst_ref=inbox.at[i, me],
            send_sem=rs_send.at[i, j], recv_sem=rs_recv.at[i, me],
            device_id={"tr": base + j}, device_id_type=MESH)

    def rs_in(i, peer):
        return pltpu.make_async_remote_copy(
            src_ref=inbox.at[i, peer], dst_ref=inbox.at[i, peer],
            send_sem=rs_send.at[i, 0], recv_sem=rs_recv.at[i, peer],
            device_id={"tr": peer}, device_id_type=MESH)

    def ag_copy(i, d):
        return pltpu.make_async_remote_copy(
            src_ref=slabs.at[i, me - base], dst_ref=slabs.at[i, me - base],
            send_sem=ag_send.at[i, d], recv_sem=ag_recv.at[i, me - base],
            device_id={"tr": lax.rem(me + d + 1, n)}, device_id_type=MESH)

    def ag_in(i, j):
        return pltpu.make_async_remote_copy(
            src_ref=slabs.at[i, j], dst_ref=slabs.at[i, j],
            send_sem=ag_send.at[i, 0], recv_sem=ag_recv.at[i, j],
            device_id={"tr": base + j}, device_id_type=MESH)

    def span(h):
        return pl.ds(h * width, width)

    def for_other_owners(body):
        for j in range(owners):
            pl.when(me != base + j)(functools.partial(body, j))

    for k in range(PASSES):
        for b in range(blocks):
            res_v[:, block(b)] = work[:, block(b)].astype(jnp.bfloat16)
        for h in range(PARTS):
            i = k * PARTS + h
            total = jnp.zeros((rows, width), jnp.float32)
            for b in range(blocks):
                total += lax.dot_general(
                    res_v[:, block(b)], sub_v[span(h), block(b)],
                    (((1,), (1,)), ((), ())), preferred_element_type=jnp.float32)
            partial[i] = total.reshape(owners, slab, width).astype(partial.dtype)

            for_other_owners(lambda j: rs_copy(i, j).start())

        def own_sum(i):
            inbox[i, me] = partial[i, me - base]
            each(n - 1, lambda d: rs_in(i, lax.rem(me + d + 1, n)).wait_recv())
            slabs[i, me - base] = jnp.sum(inbox[i].astype(jnp.float32), axis=0).astype(jnp.bfloat16)
            each(n - 1, lambda d: ag_copy(i, d).start())

        for h in range(PARTS):
            pl.when(is_owner(me))(functools.partial(own_sum, k * PARTS + h))
        for h in range(PARTS):
            i = k * PARTS + h
            for_other_owners(lambda j: ag_in(i, j).wait_recv())
            coef = jnp.concatenate(
                [slabs[i, j].astype(jnp.float32) for j in range(owners)], axis=0).astype(jnp.bfloat16)
            for b in range(blocks):
                work[:, block(b)] -= jnp.dot(
                    coef, sub_v[span(h), block(b)], preferred_element_type=jnp.float32)
                if i == PASSES * PARTS - 1:
                    pltpu.make_async_copy(work.at[:, block(b)], out.at[:, block(b)], out_sem.at[b]).start()

    per_role(close_hops)
    for i in range(PASSES * PARTS):
        for_other_owners(lambda j: rs_copy(i, j).wait_send())

        def sent():
            each(n - 1, lambda d: ag_copy(i, d).wait_send())

        pl.when(is_owner(me))(sent)
    for b in range(blocks):
        pltpu.make_async_copy(work.at[:, block(b)], out.at[:, block(b)], out_sem.at[b]).wait()


def per_device(n, roots, residual, subspace, inverses, owner_offset, listed):
    rows, cols = residual.shape
    spans = subspace.shape[0]
    blk = inverses.shape[1]
    blocks = cols // blk
    owners = min(n // 2, rows // SUBLANES)
    slab = rows // owners
    rounds = PASSES * PARTS
    hbm = pl.BlockSpec(memory_space=pl.ANY)
    smem = pl.BlockSpec(memory_space=pltpu.SMEM)
    dma = pltpu.SemaphoreType.DMA
    return pl.pallas_call(
        functools.partial(kernel, n, roots),
        out_shape=jax.ShapeDtypeStruct((rows, cols), jnp.float32),
        in_specs=[smem, smem, hbm, hbm, hbm],
        out_specs=hbm,
        scratch_shapes=[
            pltpu.VMEM((OFFS + 1, blk, blk), jnp.bfloat16),
            pltpu.VMEM((rows, cols), jnp.bfloat16),
            pltpu.VMEM((spans, cols), jnp.bfloat16),
            pltpu.VMEM((rows, cols), jnp.float32),
            pltpu.VMEM((blocks * rows, blk), jnp.bfloat16),
            pltpu.VMEM((rounds, owners, slab, spans // PARTS), LINK),
            pltpu.VMEM((rounds, n, slab, spans // PARTS), LINK),
            pltpu.VMEM((rounds, owners, slab, spans // PARTS), jnp.bfloat16),
            dma((3,)),
            dma((HOPS, CHUNKS)), dma((OFFS + 1, CHUNKS)),
            dma((OFFS + 1, CHUNKS)), dma((OFFS + 1, CHUNKS)),
            dma((rounds, owners)), dma((rounds, n)),
            dma((rounds, n)), dma((rounds, owners)),
            dma((blocks,)),
        ],
        compiler_params=pltpu.CompilerParams(collective_id=0, has_side_effects=True),
    )(owner_offset, listed, residual, subspace, inverses)


def solution(mesh):
    body = functools.partial(per_device, mesh.shape["tr"], mesh.shape["root"])
    return jax.shard_map(
        body,
        mesh=mesh,
        in_specs=(
            P("root", ("grp", "tr")),
            P(None, ("grp", "tr")),
            P(("grp", "tr"), None, None),
            P(("grp", "tr")),
            P(("grp", "tr")),
        ),
        out_specs=P("root", ("grp", "tr")),
        check_vma=False,
    )
```
